32 devices in a mesh: dp: 4 (over x, core), uly: 8 (over z, y).
Axes of the slice: x: 2, y: 2, z: 4, core: 2. Of those that a mesh axis runs over, the one named last changes fastest.
Arguments:
- queries: bfloat16 [4, 1024, 4096], P('dp', 'uly'), may hold values from -6 to 6
- key_rows: bfloat16 [4, 1024, 4096], P('dp', 'uly'), may hold values from -5 to 5
- value_rows: bfloat16 [4, 1024, 4096], P('dp', 'uly'), may hold values from -5 to 5
- out_grad: bfloat16 [4, 1024, 4096], P('dp', 'uly'), may hold values from -5 to 5
- prev_grads: bfloat16 [4, 5120, 2048], P('dp', None, 'uly'), may hold values from -1.5 to 1.5
Outputs:
- attended: bfloat16 [4, 1024, 4096], P('dp', 'uly')
- query_grad: bfloat16 [4, 1024, 4096], P('dp', 'uly')
- key_grad: bfloat16 [4, 1024, 4096], P('dp', 'uly')
- value_grad: bfloat16 [4, 1024, 4096], P('dp', 'uly')
- grad_sum: float32 [5120, 2048], P('dp', 'uly')
The draws below stay inside these ranges and needn't reach their ends.
All inputs are finite; a program needn't handle non-finite values.
Results may differ from the reference program's by a relative error of at most 0.012.
Values may be sent and summed in bfloat16 or wider, within the bound.
A program may use at most 128 MiB of HBM per device.

```python
import math
import jax
import jax.numpy as jnp
from jax import lax

D = 5120
HD = 128
HEADS = 32
SEQ = 1024
GCOLS = 2048
N_DP = 4


def drawn_pair(key):
    base_key = jax.random.fold_in(key, 7)
    query_key, key_key = jax.random.split(base_key, 2)
    width = HEADS * HD
    query_draw = jnp.clip(jax.random.normal(query_key, (N_DP, SEQ, width), jnp.float32), -5.0, 5.0)
    key_draw = jnp.clip(jax.random.normal(key_key, (N_DP, SEQ, width), jnp.float32), -5.0, 5.0)
    return (query_draw, key_draw)


def draw_queries(key, part):
    return drawn_pair(key)[0].astype(jnp.bfloat16)


def draw_key_rows(key, part):
    return drawn_pair(key)[1].astype(jnp.bfloat16)


def with_spikes(result, own_key, source, target, blocks, factor):
    def block_of(axis_at):
        return (jnp.arange(result.shape[axis_at]) // (result.shape[axis_at] // blocks)).reshape((-1,) + (1,) * (result.ndim - 1 - axis_at))

    one_side = jax.random.permutation(own_key, blocks)[block_of(target)]
    second = (block_of(target) + blocks // 2) % blocks
    return jnp.where((block_of(source) == one_side) | (block_of(source) == second), factor * result, result)


def shard_levels(key, dims, pieces, smallest, top_value):
    level = 1.0
    for dim, shards_of in pieces:
        draws = jax.random.uniform(jax.random.fold_in(jax.random.fold_in(key, 6), dim), (shards_of,), jnp.float32, smallest / len(pieces), top_value / len(pieces))
        level = level * jnp.repeat(jnp.exp(draws), dims[dim] // shards_of).reshape((-1,) + (1,) * (len(dims) - 1 - dim))
    return level


def bell_draw(key, dims, scale, bound, cuts=(), held_as=jnp.bfloat16):
    entries = scale * jax.random.normal(key, dims, jnp.float32)
    if cuts:
        entries = entries * shard_levels(key, dims, cuts, -0.22, 0.18)
    return jnp.clip(entries, -bound, bound).astype(held_as)


def gaussian_with(own_key, shape, deviation, most, cuts, heavy, held_as=jnp.bfloat16):
    entries = deviation * jax.random.normal(own_key, shape, jnp.float32)
    if cuts:
        entries = entries * shard_levels(own_key, shape, cuts, -0.22, 0.18)
    return jnp.clip(with_spikes(entries, jax.random.fold_in(own_key, 3), *heavy), -most, most).astype(held_as)


def setup_inputs(seed: int = 0) -> dict:
    keys = jax.random.split(jax.random.key(seed), 6)
    return {
        "queries": draw_queries(jax.random.fold_in(keys[5], 71), 0),
        "key_rows": draw_key_rows(jax.random.fold_in(keys[5], 71), 0),
        "value_rows": bell_draw(keys[2], (N_DP, SEQ, HEADS * HD), 1.0, 5.0, ((0, 4), (1, 8))),
        "out_grad": bell_draw(keys[3], (N_DP, SEQ, HEADS * HD), 1.0, 5.0, ((0, 4), (1, 8))),
        "prev_grads": gaussian_with(keys[4], (N_DP, D, GCOLS), 0.25, 1.5, ((0, 4), (2, 8)), (0, 1, 4, 2.0)),
    }


def attend_one(items):
    query_head, key_head, value_head, grad_head = items
    score_scale = 1.0 / math.sqrt(HD)
    scores = jnp.dot(query_head, key_head.T, preferred_element_type=jnp.float32) * score_scale
    row_max = lax.optimization_barrier(jnp.max(scores, axis=-1, keepdims=True))
    shifted = jnp.exp(scores - row_max)
    prob_rows = shifted / lax.optimization_barrier(jnp.sum(shifted, axis=-1, keepdims=True))
    prob_low = prob_rows.astype(jnp.bfloat16)
    attended = jnp.dot(prob_low, value_head, preferred_element_type=jnp.float32).astype(jnp.bfloat16)
    dprobs = jnp.dot(grad_head, value_head.T, preferred_element_type=jnp.float32)
    row_delta = lax.optimization_barrier(jnp.sum(prob_rows * dprobs, axis=-1, keepdims=True))
    dscores = (prob_rows * (dprobs - row_delta) * score_scale).astype(jnp.bfloat16)
    query_grad = jnp.dot(dscores, key_head, preferred_element_type=jnp.float32).astype(jnp.bfloat16)
    key_grad = jnp.dot(dscores.T, query_head, preferred_element_type=jnp.float32).astype(jnp.bfloat16)
    value_grad = jnp.dot(prob_low.T, grad_head, preferred_element_type=jnp.float32).astype(jnp.bfloat16)
    return (attended, query_grad, key_grad, value_grad)

def split_heads(array):
    return array.reshape(SEQ, HEADS, HD).transpose(1, 0, 2)

def join_heads(array):
    return array.transpose(1, 0, 2).reshape(SEQ, HEADS * HD)

def attend_clip(items):
    heads_in = (split_heads(items[0]), split_heads(items[1]), split_heads(items[2]), split_heads(items[3]))
    results = lax.map(attend_one, heads_in)
    return (join_heads(results[0]), join_heads(results[1]), join_heads(results[2]), join_heads(results[3]))

def reference(queries, key_rows, value_rows, out_grad, prev_grads):
    attended, query_grad, key_grad, value_grad = lax.map(attend_clip, (queries, key_rows, value_rows, out_grad))
    grad_sum = lax.optimization_barrier(jnp.sum(prev_grads.astype(jnp.float32), axis=0))
    return (attended, query_grad, key_grad, value_grad, grad_sum)
```

```python
import functools
import math

import jax
import jax.numpy as jnp
from jax import lax
from jax.experimental import pallas as pl
from jax.experimental.pallas import tpu as pltpu
from jax.sharding import PartitionSpec as P

HD = 128
VMEM_BYTES = 67043328
MESH = pl.DeviceIdType.MESH
TRANS_B = (((1,), (1,)), ((), ()))
TRANS_A = (((0,), (0,)), ((), ()))


def dot(left, right):
    return jnp.dot(left, right, preferred_element_type=jnp.float32)


def dot_tb(left, right):
    return lax.dot_general(left, right, TRANS_B, preferred_element_type=jnp.float32)


def dot_ta(left, right):
    return lax.dot_general(left, right, TRANS_A, preferred_element_type=jnp.float32)


def far_first(count):
    return sorted(range(1, count), key=lambda step: (-min(step, count - step), step))


def kernel(
    dp_count,
    uly_count,
    block_rows,
    sum_rows,
    q_ref,
    k_ref,
    v_ref,
    g_ref,
    prev_ref,
    out_o,
    out_dq,
    out_dk,
    out_dv,
    out_sum,
    held,
    made,
    dk_acc,
    dv_acc,
    grad_in,
    in_send,
    in_recv,
    out_send,
    out_recv,
    grad_send,
    grad_recv,
    ready,
):
    me_dp = lax.axis_index("dp")
    me = lax.axis_index("uly")
    heads = held.shape[0]
    tok_rows = held.shape[3]
    seq = uly_count * tok_rows
    rows = grad_in.shape[1]
    sources = (q_ref, k_ref, v_ref, g_ref)
    targets = (out_o, out_dq, out_dk, out_dv)
    dp_steps = far_first(dp_count)

    wide = uly_count // 4
    plane = me // wide
    column = lax.rem(me, wide)
    inner = (plane == 1) | (plane == 2)

    def row(of_plane, first=0):
        return [of_plane * wide + lax.rem(column + j, wide) for j in range(first, wide)]

    across = row(3 - plane)
    two_on = row(lax.rem(plane + 2, 4))
    beside = row(plane + 1 - 2 * lax.rem(plane, 2)) + row(plane, 1)
    mirror = across[0]
    far = [jnp.where(inner, b, a) for a, b in zip(across, two_on)]
    close = [jnp.where(inner, a, b) for a, b in zip(across, two_on)]

    def columns(owner, head):
        return pl.ds(pl.multiple_of((owner * heads + head) * HD, HD), HD)

    def send_input(head, peer):
        for which in range(4):
            pltpu.make_async_remote_copy(
                src_ref=sources[which].at[0, :, columns(peer, head)],
                dst_ref=held.at[head, which, me],
                send_sem=in_send,
                recv_sem=in_recv.at[head],
                device_id=(me_dp, peer),
                device_id_type=MESH,
            ).start()

    barrier = pltpu.get_barrier_semaphore()

    def greet(peer):
        pl.semaphore_signal(barrier, inc=1, device_id=(me_dp, peer), device_id_type=MESH)

    def early(head, carry):
        send_input(head, mirror)
        return carry

    @pl.when(inner)
    def _():
        greet(mirror)
        pl.semaphore_wait(barrier, 1)
        early(0, 0)
        for peer in row(3) + row(0):
            greet(peer)
        lax.fori_loop(1, heads, early, 0)
        pl.semaphore_wait(ready, 2 * wide)

    @pl.when(jnp.logical_not(inner))
    def _():
        for peer in across + row(plane, 1):
            greet(peer)
        for step in dp_steps:
            peer = lax.rem(me_dp + step, dp_count)
            pl.semaphore_signal(barrier, inc=1, device_id=(peer, me), device_id_type=MESH)
        pl.semaphore_wait(barrier, uly_count + dp_count - 2)
        for step in dp_steps:
            peer = lax.rem(me_dp + step, dp_count)
            pl.semaphore_signal(ready, inc=1, device_id=(peer, me), device_id_type=MESH)
        pl.semaphore_wait(ready, dp_count - 1)
        for peer in row(1) + row(2):
            pl.semaphore_signal(ready, inc=1, device_id=(me_dp, peer), device_id_type=MESH)

    def send_inputs(head, carry):
        @pl.when(jnp.logical_not(inner))
        def _():
            send_input(head, mirror)

        for peer in two_on + across[1:] + beside:
            send_input(head, peer)
        for which in range(4):
            pltpu.make_async_copy(
                sources[which].at[0, :, columns(me, head)],
                held.at[head, which, me],
                in_recv.at[head],
            ).start()
        return carry

    lax.fori_loop(0, heads, send_inputs, 0)

    for step in dp_steps:
        peer = lax.rem(me_dp + step, dp_count)
        pltpu.make_async_remote_copy(
            src_ref=prev_ref.at[0, pl.ds(pl.multiple_of(peer * rows, 16), rows), :],
            dst_ref=grad_in.at[me_dp],
            send_sem=grad_send,
            recv_sem=grad_recv,
            device_id=(peer, me),
            device_id_type=MESH,
        ).start()
    pltpu.make_async_copy(
        prev_ref.at[0, pl.ds(pl.multiple_of(me_dp * rows, 16), rows), :],
        grad_in.at[me_dp],
        grad_recv,
    ).start()

    sends = []
    for turn in range(6):
        for which, peers in ((turn - 1, beside), (turn, far), (turn - 2, close[::-1])):
            if 0 <= which < 4:
                sends += [(which, peer) for peer in peers]

    def send_outputs(head):
        for which, peer in sends:
            pltpu.make_async_remote_copy(
                src_ref=made.at[head, which, peer],
                dst_ref=targets[which].at[0, :, columns(me, head)],
                send_sem=out_send,
                recv_sem=out_recv.at[which],
                device_id=(me_dp, peer),
                device_id_type=MESH,
            ).start()
        for which in range(4):
            pltpu.make_async_copy(
                made.at[head, which, me],
                targets[which].at[0, :, columns(me, head)],
                out_recv.at[which],
            ).start()

    score_scale = 1.0 / math.sqrt(HD)
    per_block = block_rows // tok_rows

    def one_head(head, carry):
        pltpu.make_async_copy(held.at[head], held.at[head], in_recv.at[head]).wait()
        keys = held[head, 1].reshape(seq, HD)
        values = held[head, 2].reshape(seq, HD)
        dk_acc[...] = jnp.zeros_like(dk_acc)
        dv_acc[...] = jnp.zeros_like(dv_acc)

        def one_block(block, inner):
            first = block * per_block
            query = held[head, 0, pl.ds(first, per_block)].reshape(block_rows, HD)
            grad = held[head, 3, pl.ds(first, per_block)].reshape(block_rows, HD)
            scores = dot_tb(query, keys) * score_scale
            row_max = jnp.max(scores, axis=-1, keepdims=True)
            shifted = jnp.exp(scores - row_max)
            prob_rows = shifted * (1.0 / jnp.sum(shifted, axis=-1, keepdims=True))
            prob_low = prob_rows.astype(jnp.bfloat16)
            dprobs = dot_tb(grad, values)
            row_delta = jnp.sum(prob_rows * dprobs, axis=-1, keepdims=True)
            dscores = (prob_rows * (dprobs - row_delta) * score_scale).astype(jnp.bfloat16)
            part = (per_block, tok_rows, HD)
            made[head, 0, pl.ds(first, per_block)] = (
                dot(prob_low, values).astype(jnp.bfloat16).reshape(part)
            )
            made[head, 1, pl.ds(first, per_block)] = (
                dot(dscores, keys).astype(jnp.bfloat16).reshape(part)
            )
            dk_acc[...] += dot_ta(dscores, query)
            dv_acc[...] += dot_ta(prob_low, grad)
            return inner

        lax.fori_loop(0, uly_count // per_block, one_block, 0)
        whole = (uly_count, tok_rows, HD)
        made[head, 2] = dk_acc[...].astype(jnp.bfloat16).reshape(whole)
        made[head, 3] = dv_acc[...].astype(jnp.bfloat16).reshape(whole)

        @pl.when(head > 0)
        def _():
            send_outputs(head - 1)

        return carry

    lax.fori_loop(0, heads, one_head, 0)

    pltpu.make_async_copy(grad_in, grad_in, grad_recv).wait()

    def sum_block(block, carry):
        span = pl.ds(pl.multiple_of(block * sum_rows, 16), sum_rows)
        total = grad_in[0, span].astype(jnp.float32)
        for term in range(1, dp_count):
            total = total + grad_in[term, span].astype(jnp.float32)
        out_sum[span] = total
        return carry

    lax.fori_loop(0, rows // sum_rows, sum_block, 0)
    send_outputs(heads - 1)

    others = pl.ds(0, uly_count - 1)
    sent = held.at[:, :, others]
    pltpu.make_async_copy(sent, sent, in_send).wait()
    grad_sent = grad_in.at[pl.ds(0, dp_count - 1)]
    pltpu.make_async_copy(grad_sent, grad_sent, grad_send).wait()
    for which in range(4):
        pltpu.make_async_copy(targets[which], targets[which], out_recv.at[which]).wait()
    made_sent = made.at[:, :, others]
    pltpu.make_async_copy(made_sent, made_sent, out_send).wait()


def store_all(*refs):
    sems = refs[10]
    copies = [pltpu.make_async_copy(refs[i], refs[5 + i], sems.at[i]) for i in range(5)]
    for copy in copies:
        copy.start()
    for copy in copies:
        copy.wait()


def on_device(queries, key_rows, value_rows, out_grad, prev_grads):
    dp_count = lax.axis_size("dp")
    uly_count = lax.axis_size("uly")
    tok_rows, width = queries.shape[1:]
    heads = width // uly_count // HD
    seq = uly_count * tok_rows
    rows = prev_grads.shape[1] // dp_count
    cols = prev_grads.shape[2]
    per_block = max(1, min(uly_count, 256 // tok_rows))
    while uly_count % per_block:
        per_block -= 1
    sum_rows = math.gcd(rows, 64)
    token_shape = (1, tok_rows, width)
    grant = VMEM_BYTES - 8 * tok_rows * width - 4 * rows * cols - (1 << 19)
    token_out = pltpu.VMEM(token_shape, jnp.bfloat16)
    in_hbm = pl.BlockSpec(memory_space=pltpu.HBM)
    in_vmem = pl.BlockSpec(memory_space=pltpu.VMEM)
    results = pl.pallas_call(
        functools.partial(kernel, dp_count, uly_count, per_block * tok_rows, sum_rows),
        out_shape=(
            token_out,
            token_out,
            token_out,
            token_out,
            pltpu.VMEM((rows, cols), jnp.float32),
        ),
        in_specs=[in_hbm] * 5,
        out_specs=[in_vmem] * 5,
        scratch_shapes=[
            pltpu.VMEM((heads, 4, uly_count, tok_rows, HD), jnp.bfloat16),
            pltpu.VMEM((heads, 4, uly_count, tok_rows, HD), jnp.bfloat16),
            pltpu.VMEM((seq, HD), jnp.float32),
            pltpu.VMEM((seq, HD), jnp.float32),
            pltpu.VMEM((dp_count, rows, cols), jnp.bfloat16),
            pltpu.SemaphoreType.DMA,
            pltpu.SemaphoreType.DMA((heads,)),
            pltpu.SemaphoreType.DMA,
            pltpu.SemaphoreType.DMA((4,)),
            pltpu.SemaphoreType.DMA,
            pltpu.SemaphoreType.DMA,
            pltpu.SemaphoreType.REGULAR,
        ],
        compiler_params=pltpu.CompilerParams(
            collective_id=0, has_side_effects=True, vmem_limit_bytes=grant
        ),
        name="attend",
    )(queries, key_rows, value_rows, out_grad, prev_grads)
    return pl.pallas_call(
        store_all,
        out_shape=tuple(jax.ShapeDtypeStruct(one.shape, one.dtype) for one in results),
        in_specs=[in_vmem] * 5,
        out_specs=[in_hbm] * 5,
        scratch_shapes=[pltpu.SemaphoreType.DMA((5,))],
        compiler_params=pltpu.CompilerParams(vmem_limit_bytes=8 * 1024 * 1024),
        name="store_all",
    )(*results)


def solution(mesh):
    return jax.shard_map(
        on_device,
        mesh=mesh,
        in_specs=(
            P("dp", "uly", None),
            P("dp", "uly", None),
            P("dp", "uly", None),
            P("dp", "uly", None),
            P("dp", None, "uly"),
        ),
        out_specs=(
            P("dp", "uly", None),
            P("dp", "uly", None),
            P("dp", "uly", None),
            P("dp", "uly", None),
            P("dp", "uly"),
        ),
        check_vma=False,
    )
```

```python
import functools
import math

import jax
import jax.numpy as jnp
from jax import lax
from jax.experimental import pallas as pl
from jax.experimental.pallas import tpu as pltpu
from jax.sharding import PartitionSpec as P

HD = 128
VMEM_BYTES = 67043328
MESH = pl.DeviceIdType.MESH
TRANS_B = (((1,), (1,)), ((), ()))
TRANS_A = (((0,), (0,)), ((), ()))


def dot(left, right):
    return jnp.dot(left, right, preferred_element_type=jnp.float32)


def dot_tb(left, right):
    return lax.dot_general(left, right, TRANS_B, preferred_element_type=jnp.float32)


def dot_ta(left, right):
    return lax.dot_general(left, right, TRANS_A, preferred_element_type=jnp.float32)


def far_first(count):
    return sorted(range(1, count), key=lambda step: (-min(step, count - step), step))


def kernel(
    dp_count,
    uly_count,
    block_rows,
    sum_rows,
    q_ref,
    k_ref,
    v_ref,
    g_ref,
    prev_ref,
    out_o,
    out_dq,
    out_dk,
    out_dv,
    out_sum,
    held,
    made,
    dk_acc,
    dv_acc,
    grad_in,
    in_send,
    in_recv,
    out_send,
    out_recv,
    grad_send,
    grad_recv,
    ready,
    staged,
    stage_sem,
):
    me_dp = lax.axis_index("dp")
    me = lax.axis_index("uly")
    heads = held.shape[0]
    tok_rows = held.shape[3]
    seq = uly_count * tok_rows
    rows = grad_in.shape[1]
    sources = (q_ref, k_ref, v_ref, g_ref)
    targets = (out_o, out_dq, out_dk, out_dv)
    dp_steps = far_first(dp_count)

    wide = uly_count // 4
    plane = me // wide
    column = lax.rem(me, wide)
    inner = (plane == 1) | (plane == 2)

    mirror = (3 - plane) * wide + column
    barrier = pltpu.get_barrier_semaphore()

    def greet(peer):
        pl.semaphore_signal(barrier, inc=1, device_id=(me_dp, peer), device_id_type=MESH)

    @pl.when(inner)
    def _():
        greet(mirror)

    def row(of_plane, first=0):
        return [of_plane * wide + lax.rem(column + j, wide) for j in range(first, wide)]

    across = row(3 - plane)
    two_on = row(lax.rem(plane + 2, 4))
    beside = row(plane + 1 - 2 * lax.rem(plane, 2)) + row(plane, 1)
    far = [jnp.where(inner, b, a) for a, b in zip(across, two_on)]
    close = [jnp.where(inner, a, b) for a, b in zip(across, two_on)]

    def columns(owner, head):
        return pl.ds(pl.multiple_of((owner * heads + head) * HD, HD), HD)

    def send_input(head, peer):
        for which in range(4):
            pltpu.make_async_remote_copy(
                src_ref=sources[which].at[0, :, columns(peer, head)],
                dst_ref=held.at[head, which, me],
                send_sem=in_send,
                recv_sem=in_recv.at[head],
                device_id=(me_dp, peer),
                device_id_type=MESH,
            ).start()

    def early(head, carry):
        send_input(head, mirror)
        return carry

    @pl.when(plane == 1)
    def _():
        for which in range(4):
            pltpu.make_async_copy(
                sources[which].at[0, :, columns(mirror, 0)], staged.at[which], stage_sem
            ).start()
        pltpu.make_async_copy(staged, staged, stage_sem).wait()
        pl.semaphore_wait(barrier, 1)
        for which in range(4):
            pltpu.make_async_remote_copy(
                src_ref=staged.at[which],
                dst_ref=held.at[0, which, me],
                send_sem=in_send,
                recv_sem=in_recv.at[0],
                device_id=(me_dp, mirror),
                device_id_type=MESH,
            ).start()

    @pl.when(plane == 2)
    def _():
        pl.semaphore_wait(barrier, 1)
        early(0, 0)

    @pl.when(inner)
    def _():
        for peer in row(3) + row(0):
            greet(peer)
        lax.fori_loop(1, heads, early, 0)
        pl.semaphore_wait(ready, 2 * wide)

    @pl.when(jnp.logical_not(inner))
    def _():
        for peer in across + row(plane, 1):
            greet(peer)
        for step in dp_steps:
            peer = lax.rem(me_dp + step, dp_count)
            pl.semaphore_signal(barrier, inc=1, device_id=(peer, me), device_id_type=MESH)
        pl.semaphore_wait(barrier, uly_count + dp_count - 2)
        for step in dp_steps:
            peer = lax.rem(me_dp + step, dp_count)
            pl.semaphore_signal(ready, inc=1, device_id=(peer, me), device_id_type=MESH)
        pl.semaphore_wait(ready, dp_count - 1)
        for peer in row(1) + row(2):
            pl.semaphore_signal(ready, inc=1, device_id=(me_dp, peer), device_id_type=MESH)

    def send_inputs(head, carry):
        @pl.when(jnp.logical_not(inner))
        def _():
            send_input(head, mirror)

        for peer in two_on + across[1:] + beside:
            send_input(head, peer)
        for which in range(4):
            pltpu.make_async_copy(
                sources[which].at[0, :, columns(me, head)],
                held.at[head, which, me],
                in_recv.at[head],
            ).start()
        return carry

    lax.fori_loop(0, heads, send_inputs, 0)

    def send_grads():
        for step in dp_steps:
            peer = lax.rem(me_dp + step, dp_count)
            pltpu.make_async_remote_copy(
                src_ref=prev_ref.at[0, pl.ds(pl.multiple_of(peer * rows, 16), rows), :],
                dst_ref=grad_in.at[me_dp],
                send_sem=grad_send,
                recv_sem=grad_recv,
                device_id=(peer, me),
                device_id_type=MESH,
            ).start()
        pltpu.make_async_copy(
            prev_ref.at[0, pl.ds(pl.multiple_of(me_dp * rows, 16), rows), :],
            grad_in.at[me_dp],
            grad_recv,
        ).start()

    sends = []
    for turn in range(6):
        for which, peers in ((turn - 1, beside), (turn, far), (turn - 2, close[::-1])):
            if 0 <= which < 4:
                sends += [(which, peer) for peer in peers]

    def send_outputs(head):
        for which, peer in sends:
            pltpu.make_async_remote_copy(
                src_ref=made.at[head, which, peer],
                dst_ref=targets[which].at[0, :, columns(me, head)],
                send_sem=out_send,
                recv_sem=out_recv,
                device_id=(me_dp, peer),
                device_id_type=MESH,
            ).start()
        for which in range(4):
            pltpu.make_async_copy(
                made.at[head, which, me],
                targets[which].at[0, :, columns(me, head)],
                out_recv,
            ).start()

    score_scale = 1.0 / math.sqrt(HD)
    per_block = block_rows // tok_rows

    def one_head(head, carry):
        pltpu.make_async_copy(held.at[head], held.at[head], in_recv.at[head]).wait()
        keys = held[head, 1].reshape(seq, HD)
        values = held[head, 2].reshape(seq, HD)
        dk_acc[...] = jnp.zeros_like(dk_acc)
        dv_acc[...] = jnp.zeros_like(dv_acc)

        def one_block(block, inner):
            first = block * per_block
            query = held[head, 0, pl.ds(first, per_block)].reshape(block_rows, HD)
            grad = held[head, 3, pl.ds(first, per_block)].reshape(block_rows, HD)
            scores = dot_tb(query, keys) * score_scale
            row_max = jnp.max(scores, axis=-1, keepdims=True)
            shifted = jnp.exp(scores - row_max)
            prob_rows = shifted * (1.0 / jnp.sum(shifted, axis=-1, keepdims=True))
            prob_low = prob_rows.astype(jnp.bfloat16)
            dprobs = dot_tb(grad, values)
            row_delta = jnp.sum(prob_rows * dprobs, axis=-1, keepdims=True)
            dscores = (prob_rows * (dprobs - row_delta) * score_scale).astype(jnp.bfloat16)
            part = (per_block, tok_rows, HD)
            made[head, 0, pl.ds(first, per_block)] = (
                dot(prob_low, values).astype(jnp.bfloat16).reshape(part)
            )
            made[head, 1, pl.ds(first, per_block)] = (
                dot(dscores, keys).astype(jnp.bfloat16).reshape(part)
            )
            dk_acc[...] += dot_ta(dscores, query)
            dv_acc[...] += dot_ta(prob_low, grad)
            return inner

        lax.fori_loop(0, uly_count // per_block, one_block, 0)
        whole = (uly_count, tok_rows, HD)
        made[head, 2] = dk_acc[...].astype(jnp.bfloat16).reshape(whole)
        made[head, 3] = dv_acc[...].astype(jnp.bfloat16).reshape(whole)

        @pl.when(head > 0)
        def _():
            send_outputs(head - 1)

        @pl.when(head == min(2, heads - 1))
        def _():
            send_grads()

        return carry

    lax.fori_loop(0, heads, one_head, 0)

    pltpu.make_async_copy(grad_in, grad_in, grad_recv).wait()

    def sum_block(block, carry):
        span = pl.ds(pl.multiple_of(block * sum_rows, 16), sum_rows)
        total = grad_in[0, span].astype(jnp.float32)
        for term in range(1, dp_count):
            total = total + grad_in[term, span].astype(jnp.float32)
        out_sum[span] = total
        return carry

    lax.fori_loop(0, rows // sum_rows, sum_block, 0)
    send_outputs(heads - 1)

    others = pl.ds(0, uly_count - 1)
    sent = held.at[:, :, others]
    pltpu.make_async_copy(sent, sent, in_send).wait()
    grad_sent = grad_in.at[pl.ds(0, dp_count - 1)]
    pltpu.make_async_copy(grad_sent, grad_sent, grad_send).wait()
    pltpu.make_async_copy(made, made, out_recv).wait()
    made_sent = made.at[:, :, others]
    pltpu.make_async_copy(made_sent, made_sent, out_send).wait()


def store_all(*refs):
    sems = refs[10]
    copies = [pltpu.make_async_copy(refs[i], refs[5 + i], sems.at[i]) for i in range(5)]
    for copy in copies:
        copy.start()
    for copy in copies:
        copy.wait()


def on_device(queries, key_rows, value_rows, out_grad, prev_grads):
    dp_count = lax.axis_size("dp")
    uly_count = lax.axis_size("uly")
    tok_rows, width = queries.shape[1:]
    heads = width // uly_count // HD
    seq = uly_count * tok_rows
    rows = prev_grads.shape[1] // dp_count
    cols = prev_grads.shape[2]
    per_block = max(1, min(uly_count, 256 // tok_rows))
    while uly_count % per_block:
        per_block -= 1
    sum_rows = math.gcd(rows, 64)
    token_shape = (1, tok_rows, width)
    grant = VMEM_BYTES - 8 * tok_rows * width - 4 * rows * cols - (1 << 19)
    token_out = pltpu.VMEM(token_shape, jnp.bfloat16)
    in_hbm = pl.BlockSpec(memory_space=pltpu.HBM)
    in_vmem = pl.BlockSpec(memory_space=pltpu.VMEM)
    results = pl.pallas_call(
        functools.partial(kernel, dp_count, uly_count, per_block * tok_rows, sum_rows),
        out_shape=(
            token_out,
            token_out,
            token_out,
            token_out,
            pltpu.VMEM((rows, cols), jnp.float32),
        ),
        in_specs=[in_hbm] * 5,
        out_specs=[in_vmem] * 5,
        scratch_shapes=[
            pltpu.VMEM((heads, 4, uly_count, tok_rows, HD), jnp.bfloat16),
            pltpu.VMEM((heads, 4, uly_count, tok_rows, HD), jnp.bfloat16),
            pltpu.VMEM((seq, HD), jnp.float32),
            pltpu.VMEM((seq, HD), jnp.float32),
            pltpu.VMEM((dp_count, rows, cols), jnp.bfloat16),
            pltpu.SemaphoreType.DMA,
            pltpu.SemaphoreType.DMA((heads,)),
            pltpu.SemaphoreType.DMA,
            pltpu.SemaphoreType.DMA,
            pltpu.SemaphoreType.DMA,
            pltpu.SemaphoreType.DMA,
            pltpu.SemaphoreType.REGULAR,
            pltpu.VMEM((4, tok_rows, HD), jnp.bfloat16),
            pltpu.SemaphoreType.DMA,
        ],
        compiler_params=pltpu.CompilerParams(
            collective_id=0, has_side_effects=True, vmem_limit_bytes=grant
        ),
        name="attend",
    )(queries, key_rows, value_rows, out_grad, prev_grads)
    return pl.pallas_call(
        store_all,
        out_shape=tuple(jax.ShapeDtypeStruct(one.shape, one.dtype) for one in results),
        in_specs=[in_vmem] * 5,
        out_specs=[in_hbm] * 5,
        scratch_shapes=[pltpu.SemaphoreType.DMA((5,))],
        compiler_params=pltpu.CompilerParams(vmem_limit_bytes=8 * 1024 * 1024),
        name="store_all",
    )(*results)


def solution(mesh):
    return jax.shard_map(
        on_device,
        mesh=mesh,
        in_specs=(
            P("dp", "uly", None),
            P("dp", "uly", None),
            P("dp", "uly", None),
            P("dp", "uly", None),
            P("dp", None, "uly"),
        ),
        out_specs=(
            P("dp", "uly", None),
            P("dp", "uly", None),
            P("dp", "uly", None),
            P("dp", "uly", None),
            P("dp", "uly"),
        ),
        check_vma=False,
    )
```

```python
import functools
import math

import jax
import jax.numpy as jnp
from jax import lax
from jax.experimental import pallas as pl
from jax.experimental.pallas import tpu as pltpu
from jax.sharding import PartitionSpec as P

HD = 128
VMEM_BYTES = 67043328
MESH = pl.DeviceIdType.MESH
TRANS_B = (((1,), (1,)), ((), ()))
TRANS_A = (((0,), (0,)), ((), ()))


def dot(left, right):
    return jnp.dot(left, right, preferred_element_type=jnp.float32)


def dot_tb(left, right):
    return lax.dot_general(left, right, TRANS_B, preferred_element_type=jnp.float32)


def dot_ta(left, right):
    return lax.dot_general(left, right, TRANS_A, preferred_element_type=jnp.float32)


def far_first(count):
    return sorted(range(1, count), key=lambda step: (-min(step, count - step), step))


def kernel(
    dp_count,
    uly_count,
    block_rows,
    sum_rows,
    q_ref,
    k_ref,
    v_ref,
    g_ref,
    prev_ref,
    out_all,
    out_sum,
    held,
    made,
    dk_acc,
    dv_acc,
    grad_in,
    in_send,
    in_recv,
    out_send,
    out_recv,
    grad_send,
    grad_recv,
    ready,
):
    me_dp = lax.axis_index("dp")
    me = lax.axis_index("uly")
    heads = held.shape[0]
    tok_rows = held.shape[3]
    seq = uly_count * tok_rows
    rows = grad_in.shape[1]
    sources = (q_ref, k_ref, v_ref, g_ref)
    dp_steps = far_first(dp_count)

    wide = uly_count // 4
    plane = me // wide
    column = lax.rem(me, wide)
    inner = (plane == 1) | (plane == 2)

    def row(of_plane, first=0):
        return [of_plane * wide + lax.rem(column + j, wide) for j in range(first, wide)]

    across = row(3 - plane)
    two_on = row(lax.rem(plane + 2, 4))
    beside = row(plane + 1 - 2 * lax.rem(plane, 2)) + row(plane, 1)
    mirror = across[0]
    far = [jnp.where(inner, b, a) for a, b in zip(across, two_on)]
    close = [jnp.where(inner, a, b) for a, b in zip(across, two_on)]

    def columns(owner, head):
        return pl.ds(pl.multiple_of((owner * heads + head) * HD, HD), HD)

    def send_input(head, peer):
        for which in range(4):
            pltpu.make_async_remote_copy(
                src_ref=sources[which].at[0, :, columns(peer, head)],
                dst_ref=held.at[head, which, me],
                send_sem=in_send,
                recv_sem=in_recv.at[head],
                device_id=(me_dp, peer),
                device_id_type=MESH,
            ).start()

    barrier = pltpu.get_barrier_semaphore()

    def greet(peer):
        pl.semaphore_signal(barrier, inc=1, device_id=(me_dp, peer), device_id_type=MESH)

    def early(head, carry):
        send_input(head, mirror)
        return carry

    @pl.when(inner)
    def _():
        greet(mirror)
        pl.semaphore_wait(barrier, 1)
        early(0, 0)
        for peer in row(3) + row(0):
            greet(peer)
        lax.fori_loop(1, heads, early, 0)
        pl.semaphore_wait(ready, 2 * wide)

    @pl.when(jnp.logical_not(inner))
    def _():
        for peer in across + row(plane, 1):
            greet(peer)
        for step in dp_steps:
            peer = lax.rem(me_dp + step, dp_count)
            pl.semaphore_signal(barrier, inc=1, device_id=(peer, me), device_id_type=MESH)
        pl.semaphore_wait(barrier, uly_count + dp_count - 2)
        for step in dp_steps:
            peer = lax.rem(me_dp + step, dp_count)
            pl.semaphore_signal(ready, inc=1, device_id=(peer, me), device_id_type=MESH)
        pl.semaphore_wait(ready, dp_count - 1)
        for peer in row(1) + row(2):
            pl.semaphore_signal(ready, inc=1, device_id=(me_dp, peer), device_id_type=MESH)

    def send_inputs(head, carry):
        @pl.when(jnp.logical_not(inner))
        def _():
            send_input(head, mirror)

        for peer in two_on + across[1:] + beside:
            send_input(head, peer)
        for which in range(4):
            pltpu.make_async_copy(
                sources[which].at[0, :, columns(me, head)],
                held.at[head, which, me],
                in_recv.at[head],
            ).start()
        return carry

    lax.fori_loop(0, heads, send_inputs, 0)

    for step in dp_steps:
        peer = lax.rem(me_dp + step, dp_count)
        pltpu.make_async_remote_copy(
            src_ref=prev_ref.at[0, pl.ds(pl.multiple_of(peer * rows, 16), rows), :],
            dst_ref=grad_in.at[me_dp],
            send_sem=grad_send,
            recv_sem=grad_recv,
            device_id=(peer, me),
            device_id_type=MESH,
        ).start()
    pltpu.make_async_copy(
        prev_ref.at[0, pl.ds(pl.multiple_of(me_dp * rows, 16), rows), :],
        grad_in.at[me_dp],
        grad_recv,
    ).start()

    def send_outputs(head):
        for peer in beside[wide:] + far + beside[:wide] + close[::-1]:
            pltpu.make_async_remote_copy(
                src_ref=made.at[head, :, peer],
                dst_ref=out_all.at[:, :, columns(me, head)],
                send_sem=out_send,
                recv_sem=out_recv,
                device_id=(me_dp, peer),
                device_id_type=MESH,
            ).start()
        pltpu.make_async_copy(
            made.at[head, :, me], out_all.at[:, :, columns(me, head)], out_recv
        ).start()

    score_scale = 1.0 / math.sqrt(HD)
    per_block = block_rows // tok_rows

    def one_head(head, carry):
        pltpu.make_async_copy(held.at[head], held.at[head], in_recv.at[head]).wait()
        keys = held[head, 1].reshape(seq, HD)
        values = held[head, 2].reshape(seq, HD)
        dk_acc[...] = jnp.zeros_like(dk_acc)
        dv_acc[...] = jnp.zeros_like(dv_acc)

        def one_block(block, inner):
            first = block * per_block
            query = held[head, 0, pl.ds(first, per_block)].reshape(block_rows, HD)
            grad = held[head, 3, pl.ds(first, per_block)].reshape(block_rows, HD)
            scores = dot_tb(query, keys) * score_scale
            row_max = jnp.max(scores, axis=-1, keepdims=True)
            shifted = jnp.exp(scores - row_max)
            prob_rows = shifted * (1.0 / jnp.sum(shifted, axis=-1, keepdims=True))
            prob_low = prob_rows.astype(jnp.bfloat16)
            dprobs = dot_tb(grad, values)
            row_delta = jnp.sum(prob_rows * dprobs, axis=-1, keepdims=True)
            dscores = (prob_rows * (dprobs - row_delta) * score_scale).astype(jnp.bfloat16)
            part = (per_block, tok_rows, HD)
            made[head, 0, pl.ds(first, per_block)] = (
                dot(prob_low, values).astype(jnp.bfloat16).reshape(part)
            )
            made[head, 1, pl.ds(first, per_block)] = (
                dot(dscores, keys).astype(jnp.bfloat16).reshape(part)
            )
            dk_acc[...] += dot_ta(dscores, query)
            dv_acc[...] += dot_ta(prob_low, grad)
            return inner

        lax.fori_loop(0, uly_count // per_block, one_block, 0)
        whole = (uly_count, tok_rows, HD)
        made[head, 2] = dk_acc[...].astype(jnp.bfloat16).reshape(whole)
        made[head, 3] = dv_acc[...].astype(jnp.bfloat16).reshape(whole)

        @pl.when(head > 0)
        def _():
            send_outputs(head - 1)

        return carry

    lax.fori_loop(0, heads, one_head, 0)

    pltpu.make_async_copy(grad_in, grad_in, grad_recv).wait()

    def sum_block(block, carry):
        span = pl.ds(pl.multiple_of(block * sum_rows, 16), sum_rows)
        total = grad_in[0, span].astype(jnp.float32)
        for term in range(1, dp_count):
            total = total + grad_in[term, span].astype(jnp.float32)
        out_sum[span] = total
        return carry

    lax.fori_loop(0, rows // sum_rows, sum_block, 0)
    send_outputs(heads - 1)

    others = pl.ds(0, uly_count - 1)
    sent = held.at[:, :, others]
    pltpu.make_async_copy(sent, sent, in_send).wait()
    grad_sent = grad_in.at[pl.ds(0, dp_count - 1)]
    pltpu.make_async_copy(grad_sent, grad_sent, grad_send).wait()
    pltpu.make_async_copy(out_all, out_all, out_recv).wait()
    made_sent = made.at[:, :, others]
    pltpu.make_async_copy(made_sent, made_sent, out_send).wait()


def store_all(*refs):
    sems = refs[7]
    copies = [
        pltpu.make_async_copy(refs[0].at[i], refs[2 + i].at[0], sems.at[i]) for i in range(4)
    ]
    copies.append(pltpu.make_async_copy(refs[1], refs[6], sems.at[4]))
    for copy in copies:
        copy.start()
    for copy in copies:
        copy.wait()


def on_device(queries, key_rows, value_rows, out_grad, prev_grads):
    dp_count = lax.axis_size("dp")
    uly_count = lax.axis_size("uly")
    tok_rows, width = queries.shape[1:]
    heads = width // uly_count // HD
    seq = uly_count * tok_rows
    rows = prev_grads.shape[1] // dp_count
    cols = prev_grads.shape[2]
    per_block = max(1, min(uly_count, 256 // tok_rows))
    while uly_count % per_block:
        per_block -= 1
    sum_rows = math.gcd(rows, 64)
    grant = VMEM_BYTES - 8 * tok_rows * width - 4 * rows * cols - (1 << 19)
    in_hbm = pl.BlockSpec(memory_space=pltpu.HBM)
    in_vmem = pl.BlockSpec(memory_space=pltpu.VMEM)
    results = pl.pallas_call(
        functools.partial(kernel, dp_count, uly_count, per_block * tok_rows, sum_rows),
        out_shape=(
            pltpu.VMEM((4, tok_rows, width), jnp.bfloat16),
            pltpu.VMEM((rows, cols), jnp.float32),
        ),
        in_specs=[in_hbm] * 5,
        out_specs=[in_vmem] * 2,
        scratch_shapes=[
            pltpu.VMEM((heads, 4, uly_count, tok_rows, HD), jnp.bfloat16),
            pltpu.VMEM((heads, 4, uly_count, tok_rows, HD), jnp.bfloat16),
            pltpu.VMEM((seq, HD), jnp.float32),
            pltpu.VMEM((seq, HD), jnp.float32),
            pltpu.VMEM((dp_count, rows, cols), jnp.bfloat16),
            pltpu.SemaphoreType.DMA,
            pltpu.SemaphoreType.DMA((heads,)),
            pltpu.SemaphoreType.DMA,
            pltpu.SemaphoreType.DMA,
            pltpu.SemaphoreType.DMA,
            pltpu.SemaphoreType.DMA,
            pltpu.SemaphoreType.REGULAR,
        ],
        compiler_params=pltpu.CompilerParams(
            collective_id=0, has_side_effects=True, vmem_limit_bytes=grant
        ),
        name="attend",
    )(queries, key_rows, value_rows, out_grad, prev_grads)
    return pl.pallas_call(
        store_all,
        out_shape=(jax.ShapeDtypeStruct((1, tok_rows, width), jnp.bfloat16),) * 4
        + (jax.ShapeDtypeStruct((rows, cols), jnp.float32),),
        in_specs=[in_vmem] * 2,
        out_specs=[in_hbm] * 5,
        scratch_shapes=[pltpu.SemaphoreType.DMA((5,))],
        compiler_params=pltpu.CompilerParams(vmem_limit_bytes=8 * 1024 * 1024),
        name="store_all",
    )(*results)


def solution(mesh):
    return jax.shard_map(
        on_device,
        mesh=mesh,
        in_specs=(
            P("dp", "uly", None),
            P("dp", "uly", None),
            P("dp", "uly", None),
            P("dp", "uly", None),
            P("dp", None, "uly"),
        ),
        out_specs=(
            P("dp", "uly", None),
            P("dp", "uly", None),
            P("dp", "uly", None),
            P("dp", "uly", None),
            P("dp", "uly"),
        ),
        check_vma=False,
    )
```

```python
import functools
import math

import jax
import jax.numpy as jnp
from jax import lax
from jax.experimental import pallas as pl
from jax.experimental.pallas import tpu as pltpu
from jax.sharding import PartitionSpec as P

HD = 128
VMEM_BYTES = 67043328
MESH = pl.DeviceIdType.MESH
TRANS_B = (((1,), (1,)), ((), ()))
TRANS_A = (((0,), (0,)), ((), ()))


def dot(left, right):
    return jnp.dot(left, right, preferred_element_type=jnp.float32)


def dot_tb(left, right):
    return lax.dot_general(left, right, TRANS_B, preferred_element_type=jnp.float32)


def dot_ta(left, right):
    return lax.dot_general(left, right, TRANS_A, preferred_element_type=jnp.float32)


def far_first(count):
    return sorted(range(1, count), key=lambda step: (-min(step, count - step), step))


def kernel(
    dp_count,
    uly_count,
    block_rows,
    sum_rows,
    q_ref,
    k_ref,
    v_ref,
    g_ref,
    prev_ref,
    out_all,
    out_sum,
    held,
    made,
    dk_acc,
    dv_acc,
    grad_in,
    in_send,
    in_recv,
    out_send,
    out_recv,
    grad_send,
    grad_recv,
    ready,
):
    me_dp = lax.axis_index("dp")
    me = lax.axis_index("uly")
    heads = held.shape[0]
    tok_rows = held.shape[3]
    seq = uly_count * tok_rows
    rows = grad_in.shape[1]
    sources = (q_ref, k_ref, v_ref, g_ref)
    dp_steps = far_first(dp_count)

    wide = uly_count // 4
    plane = me // wide
    column = lax.rem(me, wide)
    inner = (plane == 1) | (plane == 2)

    mirror = (3 - plane) * wide + column
    barrier = pltpu.get_barrier_semaphore()

    def greet(peer):
        pl.semaphore_signal(barrier, inc=1, device_id=(me_dp, peer), device_id_type=MESH)

    @pl.when(inner)
    def _():
        greet(mirror)

    def row(of_plane, first=0):
        return [of_plane * wide + lax.rem(column + j, wide) for j in range(first, wide)]

    across = row(3 - plane)
    two_on = row(lax.rem(plane + 2, 4))
    beside = row(plane + 1 - 2 * lax.rem(plane, 2)) + row(plane, 1)
    far = [jnp.where(inner, b, a) for a, b in zip(across, two_on)]
    close = [jnp.where(inner, a, b) for a, b in zip(across, two_on)]

    def columns(owner, head):
        return pl.ds(pl.multiple_of((owner * heads + head) * HD, HD), HD)

    def send_input(head, peer):
        for which in range(4):
            pltpu.make_async_remote_copy(
                src_ref=sources[which].at[0, :, columns(peer, head)],
                dst_ref=held.at[head, which, me],
                send_sem=in_send,
                recv_sem=in_recv.at[head],
                device_id=(me_dp, peer),
                device_id_type=MESH,
            ).start()

    def early(head, carry):
        send_input(head, mirror)
        return carry

    @pl.when(inner)
    def _():
        pl.semaphore_wait(barrier, 1)
        early(0, 0)
        for peer in row(3) + row(0):
            greet(peer)
        lax.fori_loop(1, heads, early, 0)
        pl.semaphore_wait(ready, 2 * wide)

    @pl.when(jnp.logical_not(inner))
    def _():
        for peer in across + row(plane, 1):
            greet(peer)
        for step in dp_steps:
            peer = lax.rem(me_dp + step, dp_count)
            pl.semaphore_signal(barrier, inc=1, device_id=(peer, me), device_id_type=MESH)
        pl.semaphore_wait(barrier, uly_count + dp_count - 2)
        for step in dp_steps:
            peer = lax.rem(me_dp + step, dp_count)
            pl.semaphore_signal(ready, inc=1, device_id=(peer, me), device_id_type=MESH)
        pl.semaphore_wait(ready, dp_count - 1)
        for peer in row(1) + row(2):
            pl.semaphore_signal(ready, inc=1, device_id=(me_dp, peer), device_id_type=MESH)

    def send_inputs(head, carry):
        @pl.when(jnp.logical_not(inner))
        def _():
            send_input(head, mirror)

        for peer in two_on + across[1:] + beside:
            send_input(head, peer)
        for which in range(4):
            pltpu.make_async_copy(
                sources[which].at[0, :, columns(me, head)],
                held.at[head, which, me],
                in_recv.at[head],
            ).start()
        return carry

    lax.fori_loop(0, heads, send_inputs, 0)

    def send_grads():
        for step in dp_steps:
            peer = lax.rem(me_dp + step, dp_count)
            pltpu.make_async_remote_copy(
                src_ref=prev_ref.at[0, pl.ds(pl.multiple_of(peer * rows, 16), rows), :],
                dst_ref=grad_in.at[me_dp],
                send_sem=grad_send,
                recv_sem=grad_recv,
                device_id=(peer, me),
                device_id_type=MESH,
            ).start()
        pltpu.make_async_copy(
            prev_ref.at[0, pl.ds(pl.multiple_of(me_dp * rows, 16), rows), :],
            grad_in.at[me_dp],
            grad_recv,
        ).start()

    def send_outputs(head):
        for peer in beside[wide:] + far + beside[:wide] + close[::-1]:
            pltpu.make_async_remote_copy(
                src_ref=made.at[head, :, peer],
                dst_ref=out_all.at[:, :, columns(me, head)],
                send_sem=out_send,
                recv_sem=out_recv,
                device_id=(me_dp, peer),
                device_id_type=MESH,
            ).start()
        pltpu.make_async_copy(
            made.at[head, :, me], out_all.at[:, :, columns(me, head)], out_recv
        ).start()

    score_scale = 1.0 / math.sqrt(HD)
    per_block = block_rows // tok_rows

    def one_head(head, carry):
        pltpu.make_async_copy(held.at[head], held.at[head], in_recv.at[head]).wait()
        keys = held[head, 1].reshape(seq, HD)
        values = held[head, 2].reshape(seq, HD)
        dk_acc[...] = jnp.zeros_like(dk_acc)
        dv_acc[...] = jnp.zeros_like(dv_acc)

        def one_block(block, inner):
            first = block * per_block
            query = held[head, 0, pl.ds(first, per_block)].reshape(block_rows, HD)
            grad = held[head, 3, pl.ds(first, per_block)].reshape(block_rows, HD)
            scores = dot_tb(query, keys) * score_scale
            row_max = jnp.max(scores, axis=-1, keepdims=True)
            shifted = jnp.exp(scores - row_max)
            prob_rows = shifted * (1.0 / jnp.sum(shifted, axis=-1, keepdims=True))
            prob_low = prob_rows.astype(jnp.bfloat16)
            dprobs = dot_tb(grad, values)
            row_delta = jnp.sum(prob_rows * dprobs, axis=-1, keepdims=True)
            dscores = (prob_rows * (dprobs - row_delta) * score_scale).astype(jnp.bfloat16)
            part = (per_block, tok_rows, HD)
            made[head, 0, pl.ds(first, per_block)] = (
                dot(prob_low, values).astype(jnp.bfloat16).reshape(part)
            )
            made[head, 1, pl.ds(first, per_block)] = (
                dot(dscores, keys).astype(jnp.bfloat16).reshape(part)
            )
            dk_acc[...] += dot_ta(dscores, query)
            dv_acc[...] += dot_ta(prob_low, grad)
            return inner

        lax.fori_loop(0, uly_count // per_block, one_block, 0)
        whole = (uly_count, tok_rows, HD)
        made[head, 2] = dk_acc[...].astype(jnp.bfloat16).reshape(whole)
        made[head, 3] = dv_acc[...].astype(jnp.bfloat16).reshape(whole)

        @pl.when(head > 0)
        def _():
            send_outputs(head - 1)

        @pl.when(head == min(2, heads - 1))
        def _():
            send_grads()

        return carry

    lax.fori_loop(0, heads, one_head, 0)

    pltpu.make_async_copy(grad_in, grad_in, grad_recv).wait()

    def sum_block(block, carry):
        span = pl.ds(pl.multiple_of(block * sum_rows, 16), sum_rows)
        total = grad_in[0, span].astype(jnp.float32)
        for term in range(1, dp_count):
            total = total + grad_in[term, span].astype(jnp.float32)
        out_sum[span] = total
        return carry

    lax.fori_loop(0, rows // sum_rows, sum_block, 0)
    send_outputs(heads - 1)

    others = pl.ds(0, uly_count - 1)
    sent = held.at[:, :, others]
    pltpu.make_async_copy(sent, sent, in_send).wait()
    grad_sent = grad_in.at[pl.ds(0, dp_count - 1)]
    pltpu.make_async_copy(grad_sent, grad_sent, grad_send).wait()
    pltpu.make_async_copy(out_all, out_all, out_recv).wait()
    made_sent = made.at[:, :, others]
    pltpu.make_async_copy(made_sent, made_sent, out_send).wait()


def store_all(*refs):
    sems = refs[7]
    copies = [
        pltpu.make_async_copy(refs[0].at[i], refs[2 + i].at[0], sems.at[i]) for i in range(4)
    ]
    copies.append(pltpu.make_async_copy(refs[1], refs[6], sems.at[4]))
    for copy in copies:
        copy.start()
    for copy in copies:
        copy.wait()


def on_device(queries, key_rows, value_rows, out_grad, prev_grads):
    dp_count = lax.axis_size("dp")
    uly_count = lax.axis_size("uly")
    tok_rows, width = queries.shape[1:]
    heads = width // uly_count // HD
    seq = uly_count * tok_rows
    rows = prev_grads.shape[1] // dp_count
    cols = prev_grads.shape[2]
    per_block = max(1, min(uly_count, 256 // tok_rows))
    while uly_count % per_block:
        per_block -= 1
    sum_rows = math.gcd(rows, 64)
    grant = VMEM_BYTES - 8 * tok_rows * width - 4 * rows * cols - (1 << 19)
    in_hbm = pl.BlockSpec(memory_space=pltpu.HBM)
    in_vmem = pl.BlockSpec(memory_space=pltpu.VMEM)
    results = pl.pallas_call(
        functools.partial(kernel, dp_count, uly_count, per_block * tok_rows, sum_rows),
        out_shape=(
            pltpu.VMEM((4, tok_rows, width), jnp.bfloat16),
            pltpu.VMEM((rows, cols), jnp.float32),
        ),
        in_specs=[in_hbm] * 5,
        out_specs=[in_vmem] * 2,
        scratch_shapes=[
            pltpu.VMEM((heads, 4, uly_count, tok_rows, HD), jnp.bfloat16),
            pltpu.VMEM((heads, 4, uly_count, tok_rows, HD), jnp.bfloat16),
            pltpu.VMEM((seq, HD), jnp.float32),
            pltpu.VMEM((seq, HD), jnp.float32),
            pltpu.VMEM((dp_count, rows, cols), jnp.bfloat16),
            pltpu.SemaphoreType.DMA,
            pltpu.SemaphoreType.DMA((heads,)),
            pltpu.SemaphoreType.DMA,
            pltpu.SemaphoreType.DMA,
            pltpu.SemaphoreType.DMA,
            pltpu.SemaphoreType.DMA,
            pltpu.SemaphoreType.REGULAR,
        ],
        compiler_params=pltpu.CompilerParams(
            collective_id=0, has_side_effects=True, vmem_limit_bytes=grant
        ),
        name="attend",
    )(queries, key_rows, value_rows, out_grad, prev_grads)
    return pl.pallas_call(
        store_all,
        out_shape=(jax.ShapeDtypeStruct((1, tok_rows, width), jnp.bfloat16),) * 4
        + (jax.ShapeDtypeStruct((rows, cols), jnp.float32),),
        in_specs=[in_vmem] * 2,
        out_specs=[in_hbm] * 5,
        scratch_shapes=[pltpu.SemaphoreType.DMA((5,))],
        compiler_params=pltpu.CompilerParams(vmem_limit_bytes=8 * 1024 * 1024),
        name="store_all",
    )(*results)


def solution(mesh):
    return jax.shard_map(
        on_device,
        mesh=mesh,
        in_specs=(
            P("dp", "uly", None),
            P("dp", "uly", None),
            P("dp", "uly", None),
            P("dp", "uly", None),
            P("dp", None, "uly"),
        ),
        out_specs=(
            P("dp", "uly", None),
            P("dp", "uly", None),
            P("dp", "uly", None),
            P("dp", "uly", None),
            P("dp", "uly"),
        ),
        check_vma=False,
    )
```
